32 devices in a mesh: xz: 16 (over z, y, x), gy: 2 (over core).
Axes of the slice: x: 2, y: 2, z: 4, core: 2. Of those that a mesh axis runs over, the one named last changes fastest.
Arguments:
- initial_state: float32 [3, 2, 16, 512, 512], P(None, None, 'gy', 'xz'), may hold values from -6 to 6
- drag_rate: float32 [16, 512, 1024], P('gy', 'xz'), may hold values from 0.02 to 0.6
- wall_control: float32 [512, 1024], P('xz'), may hold values from -6 to 6
- lift_profile: float32 [16], replicated, may hold values from 0.05 to 0.3
- schur_inverse: float32 [16, 8, 512, 512], P('gy', None, 'xz'), may hold values from -1 to 3, as said below
Outputs:
- final_state: float32 [3, 2, 16, 512, 512], P(None, None, 'gy', 'xz')
- control_gradient: float32 [512, 1024], P('xz', 'gy')
The draws below stay inside these ranges and needn't reach their ends.
Inputs may be any that keep to these rules, and one draw needn't show every extreme that they name: `schur_inverse`: each 8 x 8 block of one wavenumber holds the precomputed inverse of a Schur complement; dimension 1 indexes the block's columns.
All inputs are finite; a program needn't handle non-finite values.
Results may differ from the reference program's by a relative error of at most 0.00014.
Values sent between devices are 32-bit elements; how exact they have to be, the bound alone decides.
A program may use at most 128 MiB of HBM per device.

```python
import math
import jax
import jax.numpy as jnp
from jax import lax

NX = 1024
NZ = 512
KX = 512
CY = 8
NY = 16
STEPS = 2
N_GY = 2


def draw_schur_inverse(key, part):
    subkeys = jax.random.split(key, 4)
    blocks = NY // CY
    full_shape = (blocks, CY, CY, NX // 2, NZ)
    diag_low = 0.4
    rank_weight = 0.6
    spread = 0.5
    diagonal = jax.random.uniform(subkeys[0], (blocks, CY, 1, NX // 2, NZ), jnp.float32, diag_low, 1.0)
    identity = (jnp.arange(CY)[:, None] == jnp.arange(CY)[None, :]).astype(jnp.float32)[None, :, :, None, None]
    jitter = jax.random.uniform(subkeys[1], full_shape, jnp.float32, -1.0, 1.0) * (spread / math.sqrt(CY))
    left_side = jax.random.uniform(subkeys[2], (blocks, CY, 1, NX // 2, NZ), jnp.float32, 0.5, 1.0)
    right_side = jax.random.uniform(subkeys[3], (blocks, 1, CY, NX // 2, NZ), jnp.float32, 0.5, 1.0)
    blocked = identity * diagonal + jitter + rank_weight * left_side * right_side
    stream_wave = 2.0 * math.pi / NX * jnp.arange(NX // 2).astype(jnp.float32)
    span_ids = jnp.arange(NZ)
    signed = jnp.where(span_ids < NZ // 2, span_ids, span_ids - NZ)
    span_wave = jnp.where(span_ids == NZ // 2, 0.0, 2.0 * math.pi / NZ * signed.astype(jnp.float32))
    damping = 1.0 + stream_wave[:, None] ** 2 + span_wave[None, :] ** 2
    return (blocked / damping).reshape(NY, CY, NX // 2, NZ)


def level_of(own_key, extent, cuts, least, top_value):
    gain = 1.0
    for axis_at, blocks in cuts:
        steps = jax.random.uniform(jax.random.fold_in(jax.random.fold_in(own_key, 6), axis_at), (blocks,), jnp.float32, least / len(cuts), top_value / len(cuts))
        gain = gain * jnp.repeat(jnp.exp(steps), extent[axis_at] // blocks).reshape((-1,) + (1,) * (len(extent) - 1 - axis_at))
    return gain


def gaussian(rng, shape, width, reach, cuts=(), dtype=jnp.bfloat16):
    level = level_of(rng, shape, cuts, -0.22, 0.18) if cuts else 1.0
    entries = jax.random.normal(rng, shape, jnp.float32) * width * level
    return jnp.minimum(jnp.maximum(entries, -reach), reach).astype(dtype)


def setup_inputs(seed: int = 0) -> dict:
    seeds = jax.random.split(jax.random.key(seed), 6)
    return {
        "initial_state": gaussian(seeds[0], (3, 2, NY, KX, NZ), 1.0, 6.0, ((2, 2), (3, 16)), jnp.float32),
        "drag_rate": jnp.clip(jnp.exp(math.log(0.6) - 3.4011974 * jax.random.uniform(seeds[1], (NY, NZ, NX), jnp.float32) ** level_of(seeds[1], (NY, NZ, NX), ((0, 2), (1, 16)), -0.2, 0.2)), 0.02, 0.6),
        "wall_control": gaussian(seeds[2], (NZ, NX), 1.0, 6.0, ((0, 16),), jnp.float32),
        "lift_profile": jnp.clip(jnp.exp(jax.random.uniform(seeds[3], (NY,), jnp.float32, math.log(0.05), math.log(0.3))), 0.05, 0.3),
        "schur_inverse": draw_schur_inverse(jax.random.fold_in(seeds[5], 71), 0),
    }


DIFFUSION = 0.04

def pair_rotate(spectrum, factor):
    return jnp.stack([-factor * spectrum[1], factor * spectrum[0]])

def reference(initial_state, drag_rate, wall_control, lift_profile, schur_inverse):
    mode_ids = jnp.arange(KX)
    stream_factor = (2.0 * math.pi / NX * mode_ids.astype(jnp.float32))[:, None]
    span_ids = jnp.arange(NZ)
    signed = jnp.where(span_ids < NZ // 2, span_ids, span_ids - NZ)
    span_wave = jnp.where(span_ids == NZ // 2, 0.0, 2.0 * math.pi / NZ * signed.astype(jnp.float32))
    wave_square = stream_factor ** 2 + span_wave[None, :] ** 2

    def to_physical(spectral):
        values = lax.complex(spectral[0], spectral[1])
        values = jnp.fft.ifft(values, axis=2, norm='ortho')
        values = jnp.swapaxes(values, 1, 2)
        values = jnp.pad(values, ((0, 0), (0, 0), (0, 1)))
        return jnp.fft.irfft(values, n=NX, axis=2, norm='ortho')

    def to_spectral(physical):
        values = jnp.fft.rfft(physical, axis=2, norm='ortho')[:, :, :KX]
        values = jnp.swapaxes(values, 1, 2)
        values = jnp.fft.fft(values, axis=2, norm='ortho')
        return jnp.stack([jnp.real(values), jnp.imag(values)])

    def curvature(spectrum):
        padded = jnp.pad(spectrum, ((0, 0), (1, 1), (0, 0), (0, 0)))
        return padded[:, 2:] - 2.0 * spectrum + padded[:, :-2]

    def centred(spectrum):
        padded = jnp.pad(spectrum, ((0, 0), (1, 1), (0, 0), (0, 0)))
        return (padded[:, 2:] - padded[:, :-2]) / 2.0

    def solve(source):
        running = jnp.zeros((2, KX, NZ), jnp.float32)
        partials = []
        for block_index in range(N_GY):
            matrix = schur_inverse[block_index * CY:(block_index + 1) * CY]
            values = source[:, block_index * CY:(block_index + 1) * CY]
            summed = jnp.einsum('ijkq,cjkq->cikq', matrix, values, precision=lax.Precision.HIGHEST)
            partial_value = summed + matrix[:, 0][None] * running[:, None]
            running = partial_value[:, CY - 1]
            partials.append(partial_value)
        running = jnp.zeros((2, KX, NZ), jnp.float32)
        solved = [None] * N_GY
        for block_index in reversed(range(N_GY)):
            matrix = schur_inverse[block_index * CY:(block_index + 1) * CY]
            complete = partials[block_index] + matrix[:, CY - 1][None] * running[:, None]
            running = complete[:, 0]
            solved[block_index] = complete
        return jnp.concatenate(solved, axis=1)

    def evolve(control_plane):
        control_hat = to_spectral(control_plane[None])[:, 0]
        fields = initial_state
        for section_index in range(STEPS):
            stream_part = fields[0]
            normal_part = fields[1]
            span_part = fields[2]
            drag_term = to_spectral(drag_rate * to_physical(stream_part))
            stream_star = stream_part + DIFFUSION * (curvature(stream_part) - wave_square * stream_part) - drag_term
            normal_star = normal_part + DIFFUSION * (curvature(normal_part) - wave_square * normal_part) + lift_profile[:, None, None] * control_hat[:, None]
            span_star = span_part + DIFFUSION * (curvature(span_part) - wave_square * span_part)
            divergence = pair_rotate(stream_star, stream_factor) + centred(normal_star) + pair_rotate(span_star, span_wave)
            pressure = solve(divergence)
            fields = jnp.stack([stream_star - pair_rotate(pressure, stream_factor), normal_star - centred(pressure), span_star - pair_rotate(pressure, span_wave)])
        return fields
    final_state, pullback = jax.vjp(evolve, wall_control)
    control_gradient = pullback(final_state)[0]
    return (final_state, control_gradient)
```

```python
import functools
import math

import jax
import jax.numpy as jnp
import ml_dtypes
import numpy as np
from jax import lax
from jax.experimental import pallas as pl
from jax.experimental.pallas import tpu as pltpu
from jax.sharding import PartitionSpec as P

STEPS = 2


DIFFUSION = 0.04
HIGHEST = lax.Precision.HIGHEST
MESH = pl.DeviceIdType.MESH
LANES = 128
QUAD = 4


def split_host(table):
    high = table.astype(ml_dtypes.bfloat16)
    low = (table - high.astype(np.float64)).astype(ml_dtypes.bfloat16)
    return np.stack([high, low])


def host_tables(stream_len, span_count, count):
    z = np.arange(span_count)
    angle = 2.0 * math.pi / span_count * (np.outer(z, z) % span_count)
    span = np.concatenate([np.cos(angle), np.sin(angle)], axis=1) / math.sqrt(span_count)
    n = np.arange(stream_len)
    k = np.arange(stream_len // 2)
    angle = 2.0 * math.pi / stream_len * (np.outer(k, n) % stream_len)
    stream = np.stack([np.cos(angle), -np.sin(angle)]) / math.sqrt(stream_len)
    stream = stream.reshape(2, count, -1, stream_len).transpose(1, 0, 2, 3).reshape(-1, stream_len)
    return split_host(span), split_host(stream.T.copy()), split_host(stream)


def split_pair(x):
    high = x.astype(jnp.bfloat16)
    low = (x - high.astype(jnp.float32)).astype(jnp.bfloat16)
    return high, low


def mxu(a, b):
    return jnp.dot(a, b, preferred_element_type=jnp.float32)


def span_product(x, table):
    high, low = split_pair(x)
    return mxu(high, table[0]) + (mxu(low, table[0]) + mxu(high, table[1]))


def stream_product(table, pair, store):
    tile = 256

    def body(index, carry):
        rows = pl.ds(pl.multiple_of(index * tile, tile), tile)
        wide = mxu(table[0, rows, :], pair[...])
        narrow = mxu(table[1, rows, :], pair[:, :LANES])
        store(rows, wide[:, :LANES] + (wide[:, LANES:] + narrow))
        return carry

    lax.fori_loop(0, table.shape[1] // tile, body, 0)


def swap_groups(tiles):
    a0, a1, a2, a3 = tiles
    group = lax.broadcasted_iota(jnp.int32, a0.shape, a0.ndim - 1) // (LANES // QUAD)
    lower = group < 2
    even = group % 2 == 0
    axis = a0.ndim - 1
    half = LANES // 2
    step = LANES // QUAD

    def far(x, y):
        return (
            jnp.where(lower, x, pltpu.roll(y, half, axis)),
            jnp.where(lower, pltpu.roll(x, half, axis), y),
        )

    def near(x, y):
        return (
            jnp.where(even, x, pltpu.roll(y, step, axis)),
            jnp.where(even, pltpu.roll(x, LANES - step, axis), y),
        )

    b0, b2 = far(a0, a2)
    b1, b3 = far(a1, a3)
    return near(b0, b1) + near(b2, b3)


def greet(count, me):
    barrier = pltpu.get_barrier_semaphore()

    def body(step, carry):
        peer = lax.rem(me + step, count)
        pl.semaphore_signal(barrier, inc=1, device_id={"xz": peer}, device_id_type=MESH)
        return carry

    lax.fori_loop(1, count, body, 0)
    pl.semaphore_wait(barrier, count - 1)


class Exchange:
    def __init__(self, count, me, outbox, inbox, send_sem, recv_sem):
        self.count, self.me = count, me
        self.outbox, self.inbox, self.send_sem, self.recv_sem = outbox, inbox, send_sem, recv_sem

    def copy(self, peer, slot):
        return pltpu.make_async_remote_copy(
            src_ref=self.outbox.at[peer],
            dst_ref=self.inbox.at[slot],
            send_sem=self.send_sem.at[peer],
            recv_sem=self.recv_sem.at[slot],
            device_id={"xz": peer},
            device_id_type=MESH,
        )

    def loop(self, action):
        def body(step, carry):
            action(lax.rem(self.me + step, self.count))
            return carry

        lax.fori_loop(1, self.count, body, 0)

    def start(self):
        self.loop(lambda peer: self.copy(peer, self.me).start())
        self.inbox[self.me] = self.outbox[self.me]

    def arrive(self):
        self.loop(lambda peer: self.copy(peer, peer).wait_recv())

    def finish(self):
        self.loop(lambda peer: self.copy(peer, peer).wait_send())


def drag_kernel(count, with_control, *refs):
    refs = list(refs)
    spectral, drag = refs.pop(0), refs.pop(0)
    control = refs.pop(0) if with_control else None
    span_far, inverse_far, forward_far = refs.pop(0), refs.pop(0), refs.pop(0)
    out = refs.pop(0)
    control_out = refs.pop(0) if with_control else None
    span, inverse, forward, out1, in1, out2, in2, pair, gathered, table_sem, send_sem, recv_sem = refs[:12]
    me = lax.axis_index("xz")
    chunks = drag.shape[0]
    modes, span_count = spectral.shape[2], spectral.shape[3]
    block = QUAD * modes
    groups = count // QUAD
    loads = [
        pltpu.make_async_copy(far, near, table_sem.at[i])
        for i, (far, near) in enumerate(((span_far, span), (inverse_far, inverse), (forward_far, forward)))
    ]
    for load in loads:
        load.start()
    greet(count, me)
    loads[0].wait()
    first = [Exchange(count, me, out1.at[g], in1.at[g], send_sem.at[0, g], recv_sem.at[0, g]) for g in range(chunks)]
    second = [Exchange(count, me, out2.at[g], in2.at[g], send_sem.at[1, g], recv_sem.at[1, g]) for g in range(chunks)]
    for g in range(chunks):
        x = spectral[:, QUAD * g : QUAD * (g + 1)].reshape(2 * block, span_count)
        w = span_product(x, span)
        halfway = (
            w[:block, :span_count] - w[block:, span_count:],
            w[:block, span_count:] + w[block:, :span_count],
        )
        for part in range(2):
            for h in range(groups):
                lanes = slice(LANES * h, LANES * (h + 1))
                tiles = [halfway[part][modes * y : modes * (y + 1), lanes] for y in range(QUAD)]
                for i, tile in enumerate(swap_groups(tiles)):
                    out1[g, QUAD * h + i, part] = tile
        first[g].start()
    loads[1].wait()
    loads[2].wait()
    if with_control:
        outc, inc, sendc_sem, recvc_sem = refs[12:]
        narrow = modes // QUAD
        third = Exchange(count, me, outc, inc, sendc_sem, recvc_sem)
        high, low = split_pair(control[...])
        pair[:, :LANES] = high
        pair[:, LANES:] = low
        owners = 256 // (2 * modes)

        def pack(rows, y):
            base = rows.start // (2 * modes)
            y = y.reshape(owners, 2, modes, LANES)
            for s in range(owners):
                for part in range(2):
                    tile = y[s, part]
                    moved = tile[:narrow]
                    group = lax.broadcasted_iota(jnp.int32, moved.shape, 1) // (LANES // QUAD)
                    for j in range(1, QUAD):
                        shifted = pltpu.roll(tile[narrow * j : narrow * (j + 1)], j * LANES // QUAD, 1)
                        moved = jnp.where(group == j, shifted, moved)
                    outc[base + s, part] = moved

        stream_product(forward, pair, pack)
        third.start()
    for g in range(chunks):
        first[g].arrive()
        high, low = split_pair(in1[g].reshape(-1, LANES))
        pair[:, :LANES] = high
        pair[:, LANES:] = low

        def damp(rows, physical):
            gathered[rows, :] = physical * drag[g, rows, :]

        stream_product(inverse, pair, damp)
        high, low = split_pair(gathered[...])
        pair[:, :LANES] = high
        pair[:, LANES:] = low
        owners = 256 // (2 * modes)

        def send_rows(rows, y):
            out2[g, pl.ds(rows.start // (2 * modes), owners)] = y.reshape(owners, 2, modes, LANES)

        stream_product(forward, pair, send_rows)
        second[g].start()
    if with_control:
        third.arrive()
        parts = []
        for part in range(2):
            columns = []
            for h in range(groups):
                tiles = [inc[QUAD * h + i, part] for i in range(QUAD)]
                columns.append(jnp.concatenate(swap_groups(tiles), axis=0))
            parts.append(jnp.concatenate(columns, axis=1))
        w = span_product(jnp.concatenate(parts, axis=0), span)
        control_out[0] = w[:modes, :span_count] + w[modes:, span_count:]
        control_out[1] = w[modes:, :span_count] - w[:modes, span_count:]
    for g in range(chunks):
        second[g].arrive()
        parts = []
        for part in range(2):
            columns = []
            for h in range(groups):
                tiles = [in2[g, QUAD * h + i, part] for i in range(QUAD)]
                columns.append(jnp.concatenate(swap_groups(tiles), axis=0))
            parts.append(jnp.concatenate(columns, axis=1))
        w = span_product(jnp.concatenate(parts, axis=0), span)
        out[0, QUAD * g : QUAD * (g + 1)] = (w[:block, :span_count] + w[block:, span_count:]).reshape(
            QUAD, modes, span_count
        )
        out[1, QUAD * g : QUAD * (g + 1)] = (w[block:, :span_count] - w[:block, span_count:]).reshape(
            QUAD, modes, span_count
        )
    for exchange in first + second + ([third] if with_control else []):
        exchange.finish()


def plane_kernel(count, spectral, span_far, inverse_far, out, span, inverse, outbox, inbox, pair, table_sem, send_sem, recv_sem):
    me = lax.axis_index("xz")
    modes, span_count = spectral.shape[1], spectral.shape[2]
    groups = count // QUAD
    narrow = modes // QUAD
    loads = [
        pltpu.make_async_copy(span_far, span, table_sem.at[0]),
        pltpu.make_async_copy(inverse_far, inverse, table_sem.at[1]),
    ]
    for load in loads:
        load.start()
    greet(count, me)
    loads[0].wait()
    exchange = Exchange(count, me, outbox, inbox, send_sem, recv_sem)
    w = span_product(spectral[...].reshape(2 * modes, span_count), span)
    halfway = (
        w[:modes, :span_count] - w[modes:, span_count:],
        w[:modes, span_count:] + w[modes:, :span_count],
    )
    for part in range(2):
        for h in range(groups):
            lanes = slice(LANES * h, LANES * (h + 1))
            tiles = [halfway[part][narrow * j : narrow * (j + 1), lanes] for j in range(QUAD)]
            for i, tile in enumerate(swap_groups(tiles)):
                outbox[QUAD * h + i, part] = tile
    exchange.start()
    loads[1].wait()
    exchange.arrive()
    for s in range(count):
        for part in range(2):
            tile = inbox[s, part]
            column = [tile] + [pltpu.roll(tile, LANES - j * LANES // QUAD, 1) for j in range(1, QUAD)]
            high, low = split_pair(jnp.concatenate(column, axis=0))
            first_row = (s * 2 + part) * modes
            pair[first_row : first_row + modes, :LANES] = high
            pair[first_row : first_row + modes, LANES:] = low

    def keep(rows, physical):
        out[rows, :] = physical

    stream_product(inverse, pair, keep)
    exchange.finish()


VMEM = pl.BlockSpec(memory_space=pltpu.VMEM)
FAR = pl.BlockSpec(memory_space=pl.ANY)


def kernel_transforms(count, rows, modes, span_count, stream_len):
    span, inverse, forward = host_tables(stream_len, span_count, count)
    chunks = rows // QUAD
    narrow = modes // QUAD

    def drag_call(spectral, drag_tiles, control=None):
        with_control = control is not None
        box = (chunks, count, 2, modes, LANES)
        shapes = [jax.ShapeDtypeStruct(spectral.shape, jnp.float32)]
        scratch = [
            pltpu.VMEM(span.shape, jnp.bfloat16),
            pltpu.VMEM(inverse.shape, jnp.bfloat16),
            pltpu.VMEM(forward.shape, jnp.bfloat16),
            pltpu.VMEM(box, jnp.float32),
            pltpu.VMEM(box, jnp.float32),
            pltpu.VMEM(box, jnp.float32),
            pltpu.VMEM(box, jnp.float32),
            pltpu.VMEM((stream_len, 2 * LANES), jnp.bfloat16),
            pltpu.VMEM((stream_len, LANES), jnp.float32),
            pltpu.SemaphoreType.DMA((3,)),
            pltpu.SemaphoreType.DMA((2, chunks, count)),
            pltpu.SemaphoreType.DMA((2, chunks, count)),
        ]
        operands = [spectral, drag_tiles]
        if with_control:
            operands.append(control)
            shapes.append(jax.ShapeDtypeStruct((2, modes, span_count), jnp.float32))
            scratch += [
                pltpu.VMEM((count, 2, narrow, LANES), jnp.float32),
                pltpu.VMEM((count, 2, narrow, LANES), jnp.float32),
                pltpu.SemaphoreType.DMA((count,)),
                pltpu.SemaphoreType.DMA((count,)),
            ]
        result = pl.pallas_call(
            functools.partial(drag_kernel, count, with_control),
            out_shape=shapes,
            in_specs=[VMEM] * len(operands) + [FAR] * 3,
            out_specs=[VMEM] * len(shapes),
            scratch_shapes=scratch,
            compiler_params=pltpu.CompilerParams(
                collective_id=1 if with_control else 0,
                has_side_effects=True,
                vmem_limit_bytes=40 * 1024 * 1024,
            ),
            cost_estimate=pl.CostEstimate(flops=20_000_000_000, bytes_accessed=16_000_000, transcendentals=0),
        )(*operands, span, inverse, forward)
        return result if with_control else result[0]

    def plane_call(spectral):
        return pl.pallas_call(
            functools.partial(plane_kernel, count),
            out_shape=jax.ShapeDtypeStruct((stream_len, LANES), jnp.float32),
            in_specs=[VMEM] + [FAR] * 2,
            out_specs=VMEM,
            scratch_shapes=[
                pltpu.VMEM(span.shape, jnp.bfloat16),
                pltpu.VMEM(inverse.shape, jnp.bfloat16),
                pltpu.VMEM((count, 2, narrow, LANES), jnp.float32),
                pltpu.VMEM((count, 2, narrow, LANES), jnp.float32),
                pltpu.VMEM((stream_len, 2 * LANES), jnp.bfloat16),
                pltpu.SemaphoreType.DMA((2,)),
                pltpu.SemaphoreType.DMA((count,)),
                pltpu.SemaphoreType.DMA((count,)),
            ],
            compiler_params=pltpu.CompilerParams(
                collective_id=2, has_side_effects=True, vmem_limit_bytes=32 * 1024 * 1024
            ),
            cost_estimate=pl.CostEstimate(flops=2_000_000_000, bytes_accessed=8_000_000, transcendentals=0),
        )(spectral, span, inverse)

    def begin(drag_rate, control):
        tiles = drag_rate.reshape(chunks, QUAD, -1, stream_len).transpose(0, 3, 1, 2)
        tiles = tiles.reshape(chunks, stream_len, LANES)
        wide = jnp.pad(control.T, ((0, 0), (0, LANES - control.shape[0])))
        return (lambda s: drag_call(s, tiles)), (lambda s: drag_call(s, tiles, wide))

    def plane(spectral):
        return plane_call(spectral)[:, : LANES // QUAD].T

    return begin, plane


def phase_pair(outer_size, inner_size, period, factor):
    outer_ids = jnp.arange(outer_size, dtype=jnp.int32)[:, None]
    inner_ids = jnp.arange(inner_size, dtype=jnp.int32)[None, :]
    angle = 2.0 * math.pi / period * (outer_ids * inner_ids % period).astype(jnp.float32)
    return (jnp.cos(angle) * factor, jnp.sin(angle) * factor)


def plain_transforms(count, rows, modes, span_count, stream_len):
    half_len = stream_len // 2
    cos_x, sin_x = phase_pair(stream_len, half_len, stream_len, 1.0 / math.sqrt(stream_len))
    cos_z, sin_z = phase_pair(span_count, span_count, span_count, 1.0 / math.sqrt(span_count))

    def to_spectral(physical):
        real_half = jnp.einsum("yzn,nk->yzk", physical, cos_x, precision=HIGHEST)
        imag_half = -jnp.einsum("yzn,nk->yzk", physical, sin_x, precision=HIGHEST)
        halfway = jnp.stack([real_half, imag_half])
        pieces = lax.all_to_all(halfway, "xz", split_axis=3, concat_axis=2, tiled=True)
        with_cos = jnp.einsum("cyzk,zq->cykq", pieces, cos_z, precision=HIGHEST)
        with_sin = jnp.einsum("cyzk,zq->cykq", pieces, sin_z, precision=HIGHEST)
        return jnp.stack([with_cos[0] + with_sin[1], with_cos[1] - with_sin[0]])

    def to_physical(spectral):
        with_cos = jnp.einsum("cykq,qz->cykz", spectral, cos_z, precision=HIGHEST)
        with_sin = jnp.einsum("cykq,qz->cykz", spectral, sin_z, precision=HIGHEST)
        halfway = jnp.stack([with_cos[0] - with_sin[1], with_sin[0] + with_cos[1]])
        pieces = lax.all_to_all(halfway, "xz", split_axis=3, concat_axis=2, tiled=True)
        return jnp.einsum("ykz,nk->yzn", pieces[0], cos_x, precision=HIGHEST) - jnp.einsum(
            "ykz,nk->yzn", pieces[1], sin_x, precision=HIGHEST
        )

    def begin(drag_rate, control):
        def drag_map(s):
            return to_spectral(drag_rate * to_physical(s))

        return drag_map, (lambda s: (drag_map(s), to_spectral(control[None])[:, 0]))

    def plane(spectral):
        return to_physical(spectral[:, None])[0]

    return begin, plane


def rotate(spectrum, factor):
    return jnp.stack([-factor * spectrum[1], factor * spectrum[0]])


def per_device(initial_state, drag_rate, wall_control, lift_profile, schur_inverse):
    row_count = initial_state.shape[2]
    mode_count = initial_state.shape[3]
    span_count = initial_state.shape[4]
    stream_len = drag_rate.shape[2]
    last_row = row_count - 1
    slab_count = lax.axis_size("gy")
    slab_index = lax.axis_index("gy")
    pencil_count = lax.axis_size("xz")
    pencil_index = lax.axis_index("xz")
    mode_ids = pencil_index * mode_count + jnp.arange(mode_count)
    stream_factor = (2.0 * math.pi / stream_len * mode_ids.astype(jnp.float32))[:, None]
    mode_weight = jnp.where(mode_ids == 0, 1.0, 2.0).astype(jnp.float32)[:, None]
    span_ids = jnp.arange(span_count)
    signed = jnp.where(span_ids < span_count // 2, span_ids, span_ids - span_count)
    span_wave = jnp.where(
        span_ids == span_count // 2, 0.0, 2.0 * math.pi / span_count * signed.astype(jnp.float32)
    )
    wave_square = stream_factor**2 + span_wave[None, :] ** 2
    fits = (
        QUAD * mode_count == LANES
        and QUAD * drag_rate.shape[1] == LANES
        and row_count % QUAD == 0
        and pencil_count % QUAD == 0
        and stream_len % 256 == 0
    )
    build = kernel_transforms if fits else plain_transforms
    begin, plane = build(pencil_count, row_count, mode_count, span_count, stream_len)
    drag_map, first_map = begin(drag_rate, wall_control)

    ends = slab_count - 1

    def from_above(tail):
        return lax.ppermute(tail, "gy", [(i, i + 1) for i in range(ends)])

    def from_below(head):
        return lax.ppermute(head, "gy", [(i + 1, i) for i in range(ends)])

    def every_slab(values):
        if slab_count == 2:
            other = lax.ppermute(values, "gy", [(0, 1), (1, 0)])
            return [jnp.where(slab_index == 0, values, other), jnp.where(slab_index == 0, other, values)]
        gathered = lax.all_gather(values, "gy", axis=0)
        return [gathered[i] for i in range(slab_count)]

    has_above = (slab_index > 0).astype(jnp.float32)
    has_below = (slab_index < slab_count - 1).astype(jnp.float32)
    corners = every_slab(
        jnp.stack(
            [
                schur_inverse[0, 0],
                schur_inverse[0, last_row],
                schur_inverse[last_row, 0],
                schur_inverse[last_row, last_row],
            ]
        )
    )
    corner_above = jnp.zeros_like(corners[0][3])
    for member in range(slab_count - 1):
        corner_above = jnp.where(slab_index == member + 1, corners[member][3], corner_above)

    padded_lift = jnp.pad(lift_profile, 1)
    lift_near = lax.dynamic_slice_in_dim(padded_lift, slab_index * row_count, row_count + 2)
    lift_own = lift_near[1 : row_count + 1]

    def halos(fields):
        tail = jnp.concatenate([fields[0, :, last_row:], fields[1, :, last_row - 1 :], fields[2, :, last_row:]], axis=1)
        head = jnp.concatenate([fields[0, :, :1], fields[1, :, :2], fields[2, :, :1]], axis=1)
        return from_above(tail), from_below(head)

    def smooth(wide):
        own = wide[:, 1:-1]
        laplace = wide[:, 2:] - 2.0 * own + wide[:, :-2]
        return own + DIFFUSION * (laplace - wave_square * own)

    def slope(wide):
        return 0.5 * (wide[:, 2:] - wide[:, :-2])

    def advance(fields, drag_term, control_hat):
        above, below = halos(fields)
        stream_star = smooth(jnp.concatenate([above[:, 0:1], fields[0], below[:, 0:1]], axis=1)) - drag_term
        span_star = smooth(jnp.concatenate([above[:, 3:4], fields[2], below[:, 3:4]], axis=1))
        normal_wide = smooth(jnp.concatenate([above[:, 1:3], fields[1], below[:, 1:3]], axis=1))
        if control_hat is not None:
            normal_wide = normal_wide + lift_near[:, None, None] * control_hat[:, None]
        normal_wide = jnp.concatenate(
            [has_above * normal_wide[:, :1], normal_wide[:, 1:-1], has_below * normal_wide[:, -1:]], axis=1
        )
        return stream_star, normal_wide[:, 1:-1], span_star, slope(normal_wide)

    def apply_blocks(values, transposed):
        summed = None
        for column in range(row_count):
            factor = schur_inverse[column] if transposed else schur_inverse[:, column]
            term = factor[None] * values[:, column : column + 1]
            summed = term if summed is None else summed + term
        return summed

    def solve(source, transposed):
        if transposed:
            first_column, last_column = schur_inverse[0], schur_inverse[last_row]
            ratio_at, turn_at = 1, 2
        else:
            first_column, last_column = schur_inverse[:, 0], schur_inverse[:, last_row]
            ratio_at, turn_at = 2, 1
        direct = apply_blocks(source, transposed)
        rims = every_slab(jnp.stack([direct[:, 0], direct[:, last_row]]))
        running = jnp.zeros_like(direct[:, 0])
        before = []
        for member in range(slab_count):
            before.append(running)
            running = rims[member][1] + corners[member][ratio_at][None] * running
        running = jnp.zeros_like(direct[:, 0])
        behind = [running] * slab_count
        for member in reversed(range(slab_count)):
            behind[member] = running
            top = rims[member][0] + corners[member][0][None] * before[member]
            running = top + corners[member][turn_at][None] * running
        entering, leaving = before[0], behind[0]
        for member in range(1, slab_count):
            entering = jnp.where(slab_index == member, before[member], entering)
            leaving = jnp.where(slab_index == member, behind[member], leaving)
        pressure = direct + first_column[None] * entering[:, None] + last_column[None] * leaving[:, None]
        row_above = entering + corner_above[None] * pressure[:, 0]
        return jnp.concatenate([row_above[:, None], pressure, leaving[:, None]], axis=1)

    def project(stream_part, normal_part, span_part, normal_slope, transposed):
        divergence = rotate(stream_part, stream_factor) + normal_slope + rotate(span_part, span_wave)
        wide = solve(divergence, transposed)
        pressure = wide[:, 1:-1]
        return jnp.stack(
            [
                stream_part - rotate(pressure, stream_factor),
                normal_part - slope(wide),
                span_part - rotate(pressure, span_wave),
            ]
        )

    fields = initial_state
    control_hat = None
    for section_index in range(STEPS):
        weighted = mode_weight * fields[0]
        if section_index == 0:
            drag_term, control_hat = first_map(weighted)
        else:
            drag_term = drag_map(weighted)
        fields = project(*advance(fields, drag_term, control_hat), False)
    final = fields
    normal_slope = slope(
        jnp.concatenate([from_above(final[1, :, last_row:]), final[1], from_below(final[1, :, :1])], axis=1)
    )
    parts = (final[0], final[1], final[2], normal_slope)
    wall_sum = jnp.zeros_like(control_hat)
    for section_index in range(STEPS):
        projected = project(*parts, True)
        wall_sum = wall_sum + jnp.sum(lift_own[:, None, None] * projected[1], axis=1)
        if section_index + 1 < STEPS:
            parts = advance(projected, mode_weight * drag_map(projected[0]), None)
    control_gradient = lax.psum_scatter(plane(wall_sum), "gy", scatter_dimension=1, tiled=True)
    return (final, control_gradient)


def solution(mesh):
    return jax.shard_map(
        per_device,
        mesh=mesh,
        in_specs=(
            P(None, None, "gy", "xz", None),
            P("gy", "xz", None),
            P("xz", None),
            P(),
            P("gy", None, "xz", None),
        ),
        out_specs=(P(None, None, "gy", "xz", None), P("xz", "gy")),
        check_vma=False,
    )
```

```python
import functools
import math

import jax
import jax.numpy as jnp
import ml_dtypes
import numpy as np
from jax import lax
from jax.experimental import pallas as pl
from jax.experimental.pallas import tpu as pltpu
from jax.sharding import PartitionSpec as P

STEPS = 2


DIFFUSION = 0.04
HIGHEST = lax.Precision.HIGHEST
MESH = pl.DeviceIdType.MESH
LANES = 128
QUAD = 4
TILE = 512


def split_host(table):
    high = table.astype(ml_dtypes.bfloat16)
    low = (table - high.astype(np.float64)).astype(ml_dtypes.bfloat16)
    return np.stack([high, low])


def host_tables(stream_len, span_count, count):
    z = np.arange(span_count)
    angle = 2.0 * math.pi / span_count * (np.outer(z, z) % span_count)
    span = np.concatenate([np.cos(angle), np.sin(angle)], axis=1) / math.sqrt(span_count)
    n = np.arange(stream_len)
    k = np.arange(stream_len // 2)
    angle = 2.0 * math.pi / stream_len * (np.outer(k, n) % stream_len)
    stream = np.stack([np.cos(angle), -np.sin(angle)]) / math.sqrt(stream_len)
    stream = stream.reshape(2, count, -1, stream_len).transpose(1, 0, 2, 3).reshape(-1, stream_len)
    return split_host(span), split_host(stream.T.copy()), split_host(stream)


def split_pair(x):
    high = x.astype(jnp.bfloat16)
    low = (x - high.astype(jnp.float32)).astype(jnp.bfloat16)
    return high, low


def mxu(a, b):
    return jnp.dot(a, b, preferred_element_type=jnp.float32)


def span_product(x, table):
    high, low = split_pair(x)
    both = mxu(jnp.concatenate([high, low], axis=0), table[0])
    return both[: x.shape[0]] + (both[x.shape[0] :] + mxu(high, table[1]))


def stream_product(table, pair, store):
    def body(index, carry):
        rows = pl.ds(pl.multiple_of(index * TILE, TILE), TILE)
        wide = mxu(table[0, rows, :], pair[...])
        narrow = mxu(table[1, rows, :], pair[:, :LANES])
        store(rows, wide[:, :LANES] + (wide[:, LANES:] + narrow))
        return carry

    lax.fori_loop(0, table.shape[1] // TILE, body, 0)


def swap_groups(tiles):
    a0, a1, a2, a3 = tiles
    group = lax.broadcasted_iota(jnp.int32, a0.shape, a0.ndim - 1) // (LANES // QUAD)
    lower = group < 2
    even = group % 2 == 0
    axis = a0.ndim - 1
    half = LANES // 2
    step = LANES // QUAD

    def far(x, y):
        return (
            jnp.where(lower, x, pltpu.roll(y, half, axis)),
            jnp.where(lower, pltpu.roll(x, half, axis), y),
        )

    def near(x, y):
        return (
            jnp.where(even, x, pltpu.roll(y, step, axis)),
            jnp.where(even, pltpu.roll(x, LANES - step, axis), y),
        )

    b0, b2 = far(a0, a2)
    b1, b3 = far(a1, a3)
    return near(b0, b1) + near(b2, b3)


def greet(count, me):
    barrier = pltpu.get_barrier_semaphore()

    def body(step, carry):
        peer = lax.rem(me + step, count)
        pl.semaphore_signal(barrier, inc=1, device_id={"xz": peer}, device_id_type=MESH)
        return carry

    lax.fori_loop(1, count, body, 0)
    pl.semaphore_wait(barrier, count - 1)


class Exchange:
    def __init__(self, count, me, outbox, inbox, send_sem, recv_sem):
        self.count, self.me = count, me
        self.outbox, self.inbox, self.send_sem, self.recv_sem = outbox, inbox, send_sem, recv_sem

    def copy(self, peer, slot):
        return pltpu.make_async_remote_copy(
            src_ref=self.outbox.at[peer],
            dst_ref=self.inbox.at[slot],
            send_sem=self.send_sem.at[peer],
            recv_sem=self.recv_sem.at[slot],
            device_id={"xz": peer},
            device_id_type=MESH,
        )

    def loop(self, action):
        def body(step, carry):
            action(lax.rem(self.me + step, self.count))
            return carry

        lax.fori_loop(1, self.count, body, 0)

    def start(self):
        self.loop(lambda peer: self.copy(peer, self.me).start())
        self.inbox[self.me] = self.outbox[self.me]

    def arrive(self):
        self.loop(lambda peer: self.copy(peer, peer).wait_recv())

    def finish(self):
        self.loop(lambda peer: self.copy(peer, peer).wait_send())


def drag_kernel(count, with_control, *refs):
    refs = list(refs)
    spectral, drag = refs.pop(0), refs.pop(0)
    control = refs.pop(0) if with_control else None
    span_far, inverse_far, forward_far = refs.pop(0), refs.pop(0), refs.pop(0)
    out = refs.pop(0)
    control_out = refs.pop(0) if with_control else None
    span, inverse, forward, out1, in1, out2, in2, pair, gathered, table_sem, send_sem, recv_sem = refs[:12]
    me = lax.axis_index("xz")
    chunks = drag.shape[0]
    modes, span_count = spectral.shape[2], spectral.shape[3]
    block = QUAD * modes
    groups = count // QUAD
    loads = [
        pltpu.make_async_copy(far, near, table_sem.at[i])
        for i, (far, near) in enumerate(((span_far, span), (inverse_far, inverse), (forward_far, forward)))
    ]
    for load in loads:
        load.start()
    greet(count, me)
    loads[0].wait()
    first = [Exchange(count, me, out1.at[g], in1.at[g], send_sem.at[0, g], recv_sem.at[0, g]) for g in range(chunks)]
    second = [Exchange(count, me, out2.at[g], in2.at[g], send_sem.at[1, g], recv_sem.at[1, g]) for g in range(chunks)]
    for g in range(chunks):
        x = spectral[:, QUAD * g : QUAD * (g + 1)].reshape(2 * block, span_count)
        w = span_product(x, span)
        halfway = (
            w[:block, :span_count] - w[block:, span_count:],
            w[:block, span_count:] + w[block:, :span_count],
        )
        for part in range(2):
            for h in range(groups):
                lanes = slice(LANES * h, LANES * (h + 1))
                tiles = [halfway[part][modes * y : modes * (y + 1), lanes] for y in range(QUAD)]
                for i, tile in enumerate(swap_groups(tiles)):
                    out1[g, QUAD * h + i, part] = tile
        first[g].start()
    loads[1].wait()
    loads[2].wait()
    if with_control:
        outc, inc, sendc_sem, recvc_sem = refs[12:]
        narrow = modes // QUAD
        third = Exchange(count, me, outc, inc, sendc_sem, recvc_sem)
        high, low = split_pair(control[...])
        pair[:, :LANES] = high
        pair[:, LANES:] = low
        owners = TILE // (2 * modes)

        def pack(rows, y):
            base = rows.start // (2 * modes)
            y = y.reshape(owners, 2, modes, LANES)
            for s in range(owners):
                for part in range(2):
                    tile = y[s, part]
                    moved = tile[:narrow]
                    group = lax.broadcasted_iota(jnp.int32, moved.shape, 1) // (LANES // QUAD)
                    for j in range(1, QUAD):
                        shifted = pltpu.roll(tile[narrow * j : narrow * (j + 1)], j * LANES // QUAD, 1)
                        moved = jnp.where(group == j, shifted, moved)
                    outc[base + s, part] = moved

        stream_product(forward, pair, pack)
        third.start()
    for g in range(chunks):
        first[g].arrive()
        high, low = split_pair(in1[g].reshape(-1, LANES))
        pair[:, :LANES] = high
        pair[:, LANES:] = low

        def damp(rows, physical):
            gathered[rows, :] = physical * drag[g, rows, :]

        stream_product(inverse, pair, damp)
        high, low = split_pair(gathered[...])
        pair[:, :LANES] = high
        pair[:, LANES:] = low
        owners = TILE // (2 * modes)

        def send_rows(rows, y):
            out2[g, pl.ds(rows.start // (2 * modes), owners)] = y.reshape(owners, 2, modes, LANES)

        stream_product(forward, pair, send_rows)
        second[g].start()
    if with_control:
        third.arrive()
        parts = []
        for part in range(2):
            columns = []
            for h in range(groups):
                tiles = [inc[QUAD * h + i, part] for i in range(QUAD)]
                columns.append(jnp.concatenate(swap_groups(tiles), axis=0))
            parts.append(jnp.concatenate(columns, axis=1))
        w = span_product(jnp.concatenate(parts, axis=0), span)
        control_out[0] = w[:modes, :span_count] + w[modes:, span_count:]
        control_out[1] = w[modes:, :span_count] - w[:modes, span_count:]
    for g in range(chunks):
        second[g].arrive()
        parts = []
        for part in range(2):
            columns = []
            for h in range(groups):
                tiles = [in2[g, QUAD * h + i, part] for i in range(QUAD)]
                columns.append(jnp.concatenate(swap_groups(tiles), axis=0))
            parts.append(jnp.concatenate(columns, axis=1))
        w = span_product(jnp.concatenate(parts, axis=0), span)
        out[0, QUAD * g : QUAD * (g + 1)] = (w[:block, :span_count] + w[block:, span_count:]).reshape(
            QUAD, modes, span_count
        )
        out[1, QUAD * g : QUAD * (g + 1)] = (w[block:, :span_count] - w[:block, span_count:]).reshape(
            QUAD, modes, span_count
        )
    for exchange in first + second + ([third] if with_control else []):
        exchange.finish()


def plane_kernel(count, spectral, span_far, inverse_far, out, span, inverse, outbox, inbox, pair, table_sem, send_sem, recv_sem):
    me = lax.axis_index("xz")
    modes, span_count = spectral.shape[1], spectral.shape[2]
    groups = count // QUAD
    narrow = modes // QUAD
    loads = [
        pltpu.make_async_copy(span_far, span, table_sem.at[0]),
        pltpu.make_async_copy(inverse_far, inverse, table_sem.at[1]),
    ]
    for load in loads:
        load.start()
    greet(count, me)
    loads[0].wait()
    exchange = Exchange(count, me, outbox, inbox, send_sem, recv_sem)
    w = span_product(spectral[...].reshape(2 * modes, span_count), span)
    halfway = (
        w[:modes, :span_count] - w[modes:, span_count:],
        w[:modes, span_count:] + w[modes:, :span_count],
    )
    for part in range(2):
        for h in range(groups):
            lanes = slice(LANES * h, LANES * (h + 1))
            tiles = [halfway[part][narrow * j : narrow * (j + 1), lanes] for j in range(QUAD)]
            for i, tile in enumerate(swap_groups(tiles)):
                outbox[QUAD * h + i, part] = tile
    exchange.start()
    loads[1].wait()
    exchange.arrive()
    for s in range(count):
        for part in range(2):
            tile = inbox[s, part]
            column = [tile] + [pltpu.roll(tile, LANES - j * LANES // QUAD, 1) for j in range(1, QUAD)]
            high, low = split_pair(jnp.concatenate(column, axis=0))
            first_row = (s * 2 + part) * modes
            pair[first_row : first_row + modes, :LANES] = high
            pair[first_row : first_row + modes, LANES:] = low

    def keep(rows, physical):
        out[rows, :] = physical

    stream_product(inverse, pair, keep)
    exchange.finish()


VMEM = pl.BlockSpec(memory_space=pltpu.VMEM)
FAR = pl.BlockSpec(memory_space=pl.ANY)


def kernel_transforms(count, rows, modes, span_count, stream_len):
    span, inverse, forward = host_tables(stream_len, span_count, count)
    chunks = rows // QUAD
    narrow = modes // QUAD

    def drag_call(spectral, drag_tiles, control=None):
        with_control = control is not None
        box = (chunks, count, 2, modes, LANES)
        shapes = [jax.ShapeDtypeStruct(spectral.shape, jnp.float32)]
        scratch = [
            pltpu.VMEM(span.shape, jnp.bfloat16),
            pltpu.VMEM(inverse.shape, jnp.bfloat16),
            pltpu.VMEM(forward.shape, jnp.bfloat16),
            pltpu.VMEM(box, jnp.float32),
            pltpu.VMEM(box, jnp.float32),
            pltpu.VMEM(box, jnp.float32),
            pltpu.VMEM(box, jnp.float32),
            pltpu.VMEM((stream_len, 2 * LANES), jnp.bfloat16),
            pltpu.VMEM((stream_len, LANES), jnp.float32),
            pltpu.SemaphoreType.DMA((3,)),
            pltpu.SemaphoreType.DMA((2, chunks, count)),
            pltpu.SemaphoreType.DMA((2, chunks, count)),
        ]
        operands = [spectral, drag_tiles]
        if with_control:
            operands.append(control)
            shapes.append(jax.ShapeDtypeStruct((2, modes, span_count), jnp.float32))
            scratch += [
                pltpu.VMEM((count, 2, narrow, LANES), jnp.float32),
                pltpu.VMEM((count, 2, narrow, LANES), jnp.float32),
                pltpu.SemaphoreType.DMA((count,)),
                pltpu.SemaphoreType.DMA((count,)),
            ]
        result = pl.pallas_call(
            functools.partial(drag_kernel, count, with_control),
            out_shape=shapes,
            in_specs=[VMEM] * len(operands) + [FAR] * 3,
            out_specs=[VMEM] * len(shapes),
            scratch_shapes=scratch,
            compiler_params=pltpu.CompilerParams(
                collective_id=1 if with_control else 0,
                has_side_effects=True,
                vmem_limit_bytes=40 * 1024 * 1024,
            ),
            cost_estimate=pl.CostEstimate(flops=20_000_000_000, bytes_accessed=16_000_000, transcendentals=0),
        )(*operands, span, inverse, forward)
        return result if with_control else result[0]

    def plane_call(spectral):
        return pl.pallas_call(
            functools.partial(plane_kernel, count),
            out_shape=jax.ShapeDtypeStruct((stream_len, LANES), jnp.float32),
            in_specs=[VMEM] + [FAR] * 2,
            out_specs=VMEM,
            scratch_shapes=[
                pltpu.VMEM(span.shape, jnp.bfloat16),
                pltpu.VMEM(inverse.shape, jnp.bfloat16),
                pltpu.VMEM((count, 2, narrow, LANES), jnp.float32),
                pltpu.VMEM((count, 2, narrow, LANES), jnp.float32),
                pltpu.VMEM((stream_len, 2 * LANES), jnp.bfloat16),
                pltpu.SemaphoreType.DMA((2,)),
                pltpu.SemaphoreType.DMA((count,)),
                pltpu.SemaphoreType.DMA((count,)),
            ],
            compiler_params=pltpu.CompilerParams(
                collective_id=2, has_side_effects=True, vmem_limit_bytes=32 * 1024 * 1024
            ),
            cost_estimate=pl.CostEstimate(flops=2_000_000_000, bytes_accessed=8_000_000, transcendentals=0),
        )(spectral, span, inverse)

    def begin(drag_rate, control):
        tiles = drag_rate.reshape(chunks, QUAD, -1, stream_len).transpose(0, 3, 1, 2)
        tiles = tiles.reshape(chunks, stream_len, LANES)
        wide = jnp.pad(control.T, ((0, 0), (0, LANES - control.shape[0])))
        return (lambda s: drag_call(s, tiles)), (lambda s: drag_call(s, tiles, wide))

    def plane(spectral):
        return plane_call(spectral)[:, : LANES // QUAD].T

    return begin, plane


def phase_pair(outer_size, inner_size, period, factor):
    outer_ids = jnp.arange(outer_size, dtype=jnp.int32)[:, None]
    inner_ids = jnp.arange(inner_size, dtype=jnp.int32)[None, :]
    angle = 2.0 * math.pi / period * (outer_ids * inner_ids % period).astype(jnp.float32)
    return (jnp.cos(angle) * factor, jnp.sin(angle) * factor)


def plain_transforms(count, rows, modes, span_count, stream_len):
    half_len = stream_len // 2
    cos_x, sin_x = phase_pair(stream_len, half_len, stream_len, 1.0 / math.sqrt(stream_len))
    cos_z, sin_z = phase_pair(span_count, span_count, span_count, 1.0 / math.sqrt(span_count))

    def to_spectral(physical):
        real_half = jnp.einsum("yzn,nk->yzk", physical, cos_x, precision=HIGHEST)
        imag_half = -jnp.einsum("yzn,nk->yzk", physical, sin_x, precision=HIGHEST)
        halfway = jnp.stack([real_half, imag_half])
        pieces = lax.all_to_all(halfway, "xz", split_axis=3, concat_axis=2, tiled=True)
        with_cos = jnp.einsum("cyzk,zq->cykq", pieces, cos_z, precision=HIGHEST)
        with_sin = jnp.einsum("cyzk,zq->cykq", pieces, sin_z, precision=HIGHEST)
        return jnp.stack([with_cos[0] + with_sin[1], with_cos[1] - with_sin[0]])

    def to_physical(spectral):
        with_cos = jnp.einsum("cykq,qz->cykz", spectral, cos_z, precision=HIGHEST)
        with_sin = jnp.einsum("cykq,qz->cykz", spectral, sin_z, precision=HIGHEST)
        halfway = jnp.stack([with_cos[0] - with_sin[1], with_sin[0] + with_cos[1]])
        pieces = lax.all_to_all(halfway, "xz", split_axis=3, concat_axis=2, tiled=True)
        return jnp.einsum("ykz,nk->yzn", pieces[0], cos_x, precision=HIGHEST) - jnp.einsum(
            "ykz,nk->yzn", pieces[1], sin_x, precision=HIGHEST
        )

    def begin(drag_rate, control):
        def drag_map(s):
            return to_spectral(drag_rate * to_physical(s))

        return drag_map, (lambda s: (drag_map(s), to_spectral(control[None])[:, 0]))

    def plane(spectral):
        return to_physical(spectral[:, None])[0]

    return begin, plane


def rotate(spectrum, factor):
    return jnp.stack([-factor * spectrum[1], factor * spectrum[0]])


def per_device(initial_state, drag_rate, wall_control, lift_profile, schur_inverse):
    row_count = initial_state.shape[2]
    mode_count = initial_state.shape[3]
    span_count = initial_state.shape[4]
    stream_len = drag_rate.shape[2]
    last_row = row_count - 1
    slab_count = lax.axis_size("gy")
    slab_index = lax.axis_index("gy")
    pencil_count = lax.axis_size("xz")
    pencil_index = lax.axis_index("xz")
    mode_ids = pencil_index * mode_count + jnp.arange(mode_count)
    stream_factor = (2.0 * math.pi / stream_len * mode_ids.astype(jnp.float32))[:, None]
    mode_weight = jnp.where(mode_ids == 0, 1.0, 2.0).astype(jnp.float32)[:, None]
    span_ids = jnp.arange(span_count)
    signed = jnp.where(span_ids < span_count // 2, span_ids, span_ids - span_count)
    span_wave = jnp.where(
        span_ids == span_count // 2, 0.0, 2.0 * math.pi / span_count * signed.astype(jnp.float32)
    )
    wave_square = stream_factor**2 + span_wave[None, :] ** 2
    fits = (
        QUAD * mode_count == LANES
        and QUAD * drag_rate.shape[1] == LANES
        and row_count % QUAD == 0
        and pencil_count % QUAD == 0
        and stream_len % TILE == 0
    )
    build = kernel_transforms if fits else plain_transforms
    begin, plane = build(pencil_count, row_count, mode_count, span_count, stream_len)
    drag_map, first_map = begin(drag_rate, wall_control)

    ends = slab_count - 1

    def from_above(tail):
        return lax.ppermute(tail, "gy", [(i, i + 1) for i in range(ends)])

    def from_below(head):
        return lax.ppermute(head, "gy", [(i + 1, i) for i in range(ends)])

    def every_slab(values):
        if slab_count == 2:
            other = lax.ppermute(values, "gy", [(0, 1), (1, 0)])
            return [jnp.where(slab_index == 0, values, other), jnp.where(slab_index == 0, other, values)]
        gathered = lax.all_gather(values, "gy", axis=0)
        return [gathered[i] for i in range(slab_count)]

    has_above = (slab_index > 0).astype(jnp.float32)
    has_below = (slab_index < slab_count - 1).astype(jnp.float32)
    corners = every_slab(
        jnp.stack(
            [
                schur_inverse[0, 0],
                schur_inverse[0, last_row],
                schur_inverse[last_row, 0],
                schur_inverse[last_row, last_row],
            ]
        )
    )
    corner_above = jnp.zeros_like(corners[0][3])
    for member in range(slab_count - 1):
        corner_above = jnp.where(slab_index == member + 1, corners[member][3], corner_above)

    padded_lift = jnp.pad(lift_profile, 1)
    lift_near = lax.dynamic_slice_in_dim(padded_lift, slab_index * row_count, row_count + 2)
    lift_own = lift_near[1 : row_count + 1]

    def halos(fields):
        tail = jnp.concatenate([fields[0, :, last_row:], fields[1, :, last_row - 1 :], fields[2, :, last_row:]], axis=1)
        head = jnp.concatenate([fields[0, :, :1], fields[1, :, :2], fields[2, :, :1]], axis=1)
        return from_above(tail), from_below(head)

    def smooth(wide):
        own = wide[:, 1:-1]
        laplace = wide[:, 2:] - 2.0 * own + wide[:, :-2]
        return own + DIFFUSION * (laplace - wave_square * own)

    def slope(wide):
        return 0.5 * (wide[:, 2:] - wide[:, :-2])

    def advance(fields, drag_term, control_hat):
        above, below = halos(fields)
        stream_star = smooth(jnp.concatenate([above[:, 0:1], fields[0], below[:, 0:1]], axis=1)) - drag_term
        span_star = smooth(jnp.concatenate([above[:, 3:4], fields[2], below[:, 3:4]], axis=1))
        normal_wide = smooth(jnp.concatenate([above[:, 1:3], fields[1], below[:, 1:3]], axis=1))
        if control_hat is not None:
            normal_wide = normal_wide + lift_near[:, None, None] * control_hat[:, None]
        normal_wide = jnp.concatenate(
            [has_above * normal_wide[:, :1], normal_wide[:, 1:-1], has_below * normal_wide[:, -1:]], axis=1
        )
        return stream_star, normal_wide[:, 1:-1], span_star, slope(normal_wide)

    def apply_blocks(values, transposed):
        summed = None
        for column in range(row_count):
            factor = schur_inverse[column] if transposed else schur_inverse[:, column]
            term = factor[None] * values[:, column : column + 1]
            summed = term if summed is None else summed + term
        return summed

    def solve(source, transposed):
        if transposed:
            first_column, last_column = schur_inverse[0], schur_inverse[last_row]
            ratio_at, turn_at = 1, 2
        else:
            first_column, last_column = schur_inverse[:, 0], schur_inverse[:, last_row]
            ratio_at, turn_at = 2, 1
        direct = apply_blocks(source, transposed)
        rims = every_slab(jnp.stack([direct[:, 0], direct[:, last_row]]))
        running = jnp.zeros_like(direct[:, 0])
        before = []
        for member in range(slab_count):
            before.append(running)
            running = rims[member][1] + corners[member][ratio_at][None] * running
        running = jnp.zeros_like(direct[:, 0])
        behind = [running] * slab_count
        for member in reversed(range(slab_count)):
            behind[member] = running
            top = rims[member][0] + corners[member][0][None] * before[member]
            running = top + corners[member][turn_at][None] * running
        entering, leaving = before[0], behind[0]
        for member in range(1, slab_count):
            entering = jnp.where(slab_index == member, before[member], entering)
            leaving = jnp.where(slab_index == member, behind[member], leaving)
        pressure = direct + first_column[None] * entering[:, None] + last_column[None] * leaving[:, None]
        row_above = entering + corner_above[None] * pressure[:, 0]
        return jnp.concatenate([row_above[:, None], pressure, leaving[:, None]], axis=1)

    def project(stream_part, normal_part, span_part, normal_slope, transposed):
        divergence = rotate(stream_part, stream_factor) + normal_slope + rotate(span_part, span_wave)
        wide = solve(divergence, transposed)
        pressure = wide[:, 1:-1]
        return jnp.stack(
            [
                stream_part - rotate(pressure, stream_factor),
                normal_part - slope(wide),
                span_part - rotate(pressure, span_wave),
            ]
        )

    fields = initial_state
    control_hat = None
    for section_index in range(STEPS):
        weighted = mode_weight * fields[0]
        if section_index == 0:
            drag_term, control_hat = first_map(weighted)
        else:
            drag_term = drag_map(weighted)
        fields = project(*advance(fields, drag_term, control_hat), False)
    final = fields
    normal_slope = slope(
        jnp.concatenate([from_above(final[1, :, last_row:]), final[1], from_below(final[1, :, :1])], axis=1)
    )
    parts = (final[0], final[1], final[2], normal_slope)
    wall_sum = jnp.zeros_like(control_hat)
    for section_index in range(STEPS):
        projected = project(*parts, True)
        wall_sum = wall_sum + jnp.sum(lift_own[:, None, None] * projected[1], axis=1)
        if section_index + 1 < STEPS:
            parts = advance(projected, mode_weight * drag_map(projected[0]), None)
    share = plane(wall_sum)
    if slab_count == 2:
        half = stream_len // 2
        first, second = share[:, :half], share[:, half:]
        upper = slab_index == 0
        other = lax.ppermute(jnp.where(upper, second, first), "gy", [(0, 1), (1, 0)])
        control_gradient = jnp.where(upper, first, second) + other
    else:
        control_gradient = lax.psum_scatter(share, "gy", scatter_dimension=1, tiled=True)
    return (final, control_gradient)


def solution(mesh):
    return jax.shard_map(
        per_device,
        mesh=mesh,
        in_specs=(
            P(None, None, "gy", "xz", None),
            P("gy", "xz", None),
            P("xz", None),
            P(),
            P("gy", None, "xz", None),
        ),
        out_specs=(P(None, None, "gy", "xz", None), P("xz", "gy")),
        check_vma=False,
    )
```
